32 devices in a mesh: rep: 4 (over x, core), fsdp: 8 (over z, y).
Axes of the slice: x: 2, y: 2, z: 4, core: 2. Of those that a mesh axis runs over, the one named last changes fastest.
Arguments:
- sequence_entries: bfloat16 [160, 96, 768], P(('rep', 'fsdp')), may hold values from -6 to 6
- picture_descriptors: bfloat16 [160, 257, 1408], P(('rep', 'fsdp')), may hold values from -6 to 6
- sentence_numbering: int32 [160, 64], P(('rep', 'fsdp')), may hold values from 0 to 1, never falling along the last dimension, each value on 1 to 48 neighbouring positions
- sentence_picture_owner: int32 [320], P(('rep', 'fsdp')), may hold values from 0 to 159
- upstream_adjoint: bfloat16 [160, 96, 768], P(('rep', 'fsdp')), may hold values from -6 to 6
- attend_triple_matrix: bfloat16 [768, 2304], P('fsdp'), may hold values from -0.21875 to 0.21875
- inward_result_matrix: bfloat16 [768, 768], P('fsdp'), may hold values from -1.25 to 1.25
- inward_result_offset: bfloat16 [768], P('fsdp'), may hold values from -2 to 2
- inward_center_scale: bfloat16 [768], P('fsdp'), may hold values from 0.5 to 1.5
- inward_center_shift: bfloat16 [768], P('fsdp'), may hold values from -1 to 1
- mixing_asker_matrix: bfloat16 [768, 768], P('fsdp'), may hold values from -0.21875 to 0.21875
- visual_lookup_pairs: bfloat16 [1408, 1536], P('fsdp'), may hold values from -0.15625 to 0.15625
- mixing_result_matrix: bfloat16 [768, 768], P('fsdp'), may hold values from -3.5 to 3.5
- mixing_result_offset: bfloat16 [768], P('fsdp'), may hold values from -2 to 2
- mixing_center_scale: bfloat16 [768], P('fsdp'), may hold values from 0.5 to 1.5
- mixing_center_shift: bfloat16 [768], P('fsdp'), may hold values from -1 to 1
- widening_matrix: bfloat16 [768, 3072], P('fsdp'), may hold values from -0.21875 to 0.21875
- widening_offset: bfloat16 [3072], P('fsdp'), may hold values from -2.5 to 2.5
- narrowing_matrix: bfloat16 [3072, 768], P('fsdp'), may hold values from -0.109375 to 0.109375
- narrowing_offset: bfloat16 [768], P('fsdp'), may hold values from -2 to 2
- perceptron_center_scale: bfloat16 [768], P('fsdp'), may hold values from 0.5 to 1.5
- perceptron_center_shift: bfloat16 [768], P('fsdp'), may hold values from -1 to 1
- picture_mapping_matrix: bfloat16 [768, 256], P('fsdp'), may hold values from -0.21875 to 0.21875
- picture_vector_offset: bfloat16 [256], P('fsdp'), may hold values from -0.5 to 0.5
- sentence_mapping_matrix: bfloat16 [768, 256], P('fsdp'), may hold values from -0.21875 to 0.21875
- sentence_vector_offset: bfloat16 [256], P('fsdp'), may hold values from -1.5 to 1.5
- logit_sharpness: float32 [], replicated, may hold values from 0.025 to 0.05
Outputs:
- out: bfloat16 [160, 96, 768], P(('rep', 'fsdp'))
- incoming_sequence_adjoint: float32 [160, 96, 768], P(('rep', 'fsdp'))
- qkv_weight_grad: float32 [768, 2304], P('fsdp')
- self_out_grad: float32 [768, 768], P('fsdp')
- self_bias_grad: float32 [768], P('fsdp')
- self_gain_grad: float32 [768], P('fsdp')
- self_shift_grad: float32 [768], P('fsdp')
- cross_query_grad: float32 [768, 768], P('fsdp')
- cross_keyval_grad: float32 [1408, 1536], P('fsdp')
- cross_out_grad: float32 [768, 768], P('fsdp')
- cross_bias_grad: float32 [768], P('fsdp')
- cross_gain_grad: float32 [768], P('fsdp')
- cross_shift_grad: float32 [768], P('fsdp')
- up_weight_grad: float32 [768, 3072], P('fsdp')
- up_bias_grad: float32 [3072], P('fsdp')
- down_weight_grad: float32 [3072, 768], P('fsdp')
- down_bias_grad: float32 [768], P('fsdp')
- feed_gain_grad: float32 [768], P('fsdp')
- feed_shift_grad: float32 [768], P('fsdp')
- image_proj_grad: float32 [768, 256], P('fsdp')
- image_bias_grad: float32 [256], P('fsdp')
- text_proj_grad: float32 [768, 256], P('fsdp')
- text_bias_grad: float32 [256], P('fsdp')
- sharpness_adjoint: float32 [], replicated
The draws below stay inside these ranges and needn't reach their ends.
Inputs may be any that keep to these rules, and one draw needn't show every extreme that they name: `sentence_numbering`: in each row the caption numbers never fall and each of the 2 captions has 16 to 48 tokens.
All inputs are finite; a program needn't handle non-finite values.
Results may differ from the reference program's by a relative error of at most 0.02.
Values may be sent and summed in bfloat16 or wider, within the bound.
No kernel may reach another device: no remote copies, remote signals or barrier semaphores. Data moves between devices by JAX's collectives and lax.ppermute only.
A program may use at most 192 MiB of HBM per device.

```python
import math
import jax
import jax.numpy as jnp
import numpy as np
from jax import lax

D = 768
HEADS = 12
HEAD = 64
FF = 3072
VIS = 1408
PATCHES = 257
EMB = 256
QUERY = 32
CAP_LEN = 64
CAPS_ROW = 2
ROW_LEN = 96
ROWS = 160
IMAGES = 160
CAPTIONS = 320
N_REP = 4
N_FSDP = 8


def plant(values, rng, low, largest):
    extent = values.shape
    place = [jax.random.randint(jax.random.fold_in(rng, axis), (), 0, extent[axis]) for axis in range(len(extent))]
    values = values.at[tuple(place)].set(low)
    longest = extent.index(max(extent))
    place[longest] = (place[longest] + 1) % extent[longest]
    return values.at[tuple(place)].set(largest)


def shard_levels(rng, extent, pieces, low, high):
    level = 1.0
    for position, parts in pieces:
        heights = jax.random.uniform(jax.random.fold_in(jax.random.fold_in(rng, 6), position), (parts,), jnp.float32, low / len(pieces), high / len(pieces))
        level = level * jnp.repeat(jnp.exp(heights), extent[position] // parts).reshape((-1,) + (1,) * (len(extent) - 1 - position))
    return level


def split_up(amount, total, most, skew):
    loads = [(1 << 20) // math.isqrt(standing ** skew) + 1 for standing in range(2, amount + 1)]
    surplus, holding = total - most - (amount - 1), [1] * (amount - 1)
    while surplus > 0:
        movable = [i for i in range(amount - 1) if holding[i] < most]
        mass, remaining = sum([loads[i] for i in movable]), surplus
        for i in movable:
            addition = min(most - holding[i], max(1, remaining * loads[i] // mass), surplus)
            holding[i] = holding[i] + addition
            surplus = surplus - addition
    return np.array([most] + holding)


def ragged(rng, amount, total, most, slope):
    if amount == 2:
        one = jax.random.randint(rng, (), max(1, total - most), min(most, total - 1) + 1)
        return jnp.stack([one, total - one])
    sizes = jnp.asarray(split_up(amount, total, most, slope), jnp.int32)
    twos = (amount - 1) // 2
    giver, taker = sizes[1:1 + 2 * twos:2], sizes[2:2 + 2 * twos:2]
    margin = jnp.minimum(giver - 1, most - taker)
    shifted = jax.random.randint(jax.random.fold_in(rng, 1), (twos,), 0, 1 << 20) % (margin + 1)
    sizes = sizes.at[1:1 + 2 * twos:2].set(giver - shifted).at[2:2 + 2 * twos:2].set(taker + shifted)
    return sizes[jax.random.permutation(jax.random.fold_in(rng, 2), amount)]


def gaussian(stream_key, shape, deviation, most, cuts=(), kind=jnp.bfloat16):
    drawn = jax.random.normal(stream_key, shape, jnp.float32) * deviation
    if len(cuts) > 0:
        drawn = shard_levels(stream_key, shape, cuts, -0.22, 0.18) * drawn
    return jnp.clip(drawn, min=-most, max=most).astype(kind)


def setup_inputs(seed: int = 0) -> dict:
    key_list = jax.random.split(jax.random.key(seed), 28)
    sequence_entries = gaussian(key_list[0], (ROWS, ROW_LEN, D), 1.0, 6.0, ((0, 32),))
    picture_descriptors = gaussian(key_list[1], (ROWS, PATCHES, VIS), 1.0, 6.0, ((0, 32),))
    sentence_numbering = jax.vmap(lambda own: jnp.searchsorted(jnp.cumsum(ragged(own, CAPS_ROW, CAP_LEN, CAP_LEN * 3 // 4, 0)), jnp.arange(CAP_LEN), side="right"))(jax.random.split(key_list[2], ROWS)).reshape((ROWS, CAP_LEN)).astype(jnp.int32)
    sentence_picture_owner = plant(jax.random.randint(key_list[3], (CAPTIONS,), 0, IMAGES), jax.random.fold_in(key_list[3], 1), 0, IMAGES - 1).astype(jnp.int32)
    upstream_adjoint = gaussian(key_list[4], (ROWS, ROW_LEN, D), 1.0, 6.0, ((0, 32),))
    attend_triple_matrix = gaussian(key_list[5], (D, 3 * D), D ** -0.5, 0.21875, ((0, 8),))
    inward_result_matrix = gaussian(key_list[6], (D, D), (max(D // 32, 1)) ** -0.5, 1.25, ((0, 8),))
    inward_result_offset = gaussian(key_list[7], (D,), 0.3, 2.0, ((0, 8),))
    inward_center_scale = jnp.clip(1.0 + 0.1 * jax.random.normal(key_list[8], (D,), jnp.float32), 0.5, 1.5).astype(jnp.bfloat16)
    inward_center_shift = gaussian(key_list[9], (D,), 0.2, 1.0, ((0, 8),))
    mixing_asker_matrix = gaussian(key_list[10], (D, D), D ** -0.5, 0.21875, ((0, 8),))
    visual_lookup_pairs = gaussian(key_list[11], (VIS, 2 * D), VIS ** -0.5, 0.15625, ((0, 8),))
    mixing_result_matrix = gaussian(key_list[12], (D, D), (max(D // 256, 1)) ** -0.5, 3.5, ((0, 8),))
    mixing_result_offset = gaussian(key_list[13], (D,), 0.3, 2.0, ((0, 8),))
    mixing_center_scale = jnp.clip(1.0 + 0.1 * jax.random.normal(key_list[14], (D,), jnp.float32), 0.5, 1.5).astype(jnp.bfloat16)
    mixing_center_shift = gaussian(key_list[15], (D,), 0.2, 1.0, ((0, 8),))
    widening_matrix = gaussian(key_list[16], (D, FF), D ** -0.5, 0.21875, ((0, 8),))
    widening_offset = gaussian(key_list[17], (FF,), 0.5, 2.5, ((0, 8),))
    narrowing_matrix = gaussian(key_list[18], (FF, D), FF ** -0.5, 0.109375, ((0, 8),))
    narrowing_offset = gaussian(key_list[19], (D,), 0.3, 2.0, ((0, 8),))
    perceptron_center_scale = jnp.clip(1.0 + 0.1 * jax.random.normal(key_list[20], (D,), jnp.float32), 0.5, 1.5).astype(jnp.bfloat16)
    perceptron_center_shift = gaussian(key_list[21], (D,), 0.2, 1.0, ((0, 8),))
    picture_mapping_matrix = gaussian(key_list[22], (D, EMB), D ** -0.5, 0.21875, ((0, 8),))
    picture_vector_offset = gaussian(key_list[23], (EMB,), 0.1, 0.5, ((0, 8),))
    sentence_mapping_matrix = gaussian(key_list[24], (D, EMB), D ** -0.5, 0.21875, ((0, 8),))
    sentence_vector_offset = gaussian(key_list[25], (EMB,), 0.3, 1.5, ((0, 8),))
    logit_sharpness = jnp.clip(jax.random.uniform(key_list[26], (), jnp.float32, 0.025, 0.05), 0.025, 0.05)
    return {"sequence_entries": sequence_entries, "picture_descriptors": picture_descriptors, "sentence_numbering": sentence_numbering, "sentence_picture_owner": sentence_picture_owner, "upstream_adjoint": upstream_adjoint, "attend_triple_matrix": attend_triple_matrix, "inward_result_matrix": inward_result_matrix, "inward_result_offset": inward_result_offset, "inward_center_scale": inward_center_scale, "inward_center_shift": inward_center_shift, "mixing_asker_matrix": mixing_asker_matrix, "visual_lookup_pairs": visual_lookup_pairs, "mixing_result_matrix": mixing_result_matrix, "mixing_result_offset": mixing_result_offset, "mixing_center_scale": mixing_center_scale, "mixing_center_shift": mixing_center_shift, "widening_matrix": widening_matrix, "widening_offset": widening_offset, "narrowing_matrix": narrowing_matrix, "narrowing_offset": narrowing_offset, "perceptron_center_scale": perceptron_center_scale, "perceptron_center_shift": perceptron_center_shift, "picture_mapping_matrix": picture_mapping_matrix, "picture_vector_offset": picture_vector_offset, "sentence_mapping_matrix": sentence_mapping_matrix, "sentence_vector_offset": sentence_vector_offset, "logit_sharpness": logit_sharpness}


@jax.custom_vjp
def low(v):
    return lax.optimization_barrier(v.astype(jnp.bfloat16)).astype(jnp.float32)

@jax.custom_vjp
def low_back(v):
    return v

def low_keep(v):
    return (low(v), None)

def low_pass(kept, grad):
    return (grad,)

def back_keep(v):
    return (v, None)

def back_low(kept, grad):
    return (low(grad),)
low.defvjp(low_keep, low_pass)
low_back.defvjp(back_keep, back_low)

def project(values, matrix):
    return jnp.einsum('...d,df->...f', values, matrix, precision=lax.Precision.HIGHEST)

def layer_norm(summed, norm_gain, norm_shift):
    center = summed - lax.optimization_barrier(jnp.mean(summed, axis=-1, keepdims=True))
    spread = lax.optimization_barrier(jnp.mean(center * center, axis=-1, keepdims=True))
    return center * lax.rsqrt(spread + 1e-06) * norm_gain + norm_shift

def unit_rows(values):
    return values * lax.rsqrt(lax.optimization_barrier(jnp.sum(values * values, axis=-1, keepdims=True)) + 1e-06)

def token_kinds(sentence_numbering):
    query_kinds = jnp.zeros((sentence_numbering.shape[0], QUERY), jnp.int32)
    return jnp.concatenate([query_kinds, sentence_numbering + 1], axis=1)

def caption_picker(sentence_numbering):
    caption_ids = jnp.arange(CAPS_ROW, dtype=jnp.int32)
    starts = lax.optimization_barrier(jnp.sum((sentence_numbering[:, None, :] < caption_ids[None, :, None]).astype(jnp.int32), axis=2))
    places = jnp.arange(sentence_numbering.shape[1], dtype=jnp.int32)
    return (places[None, None, :] == starts[:, :, None]).astype(jnp.float32)

def split_heads(values):
    return values.reshape(values.shape[0], values.shape[1], HEADS, values.shape[2] // HEADS)

def attend(queries, key_rows, value_rows, allowed):
    scaling = HEAD ** (-0.5)
    scores = jnp.einsum('bqhd,bkhd->bhqk', split_heads(queries), split_heads(key_rows), precision=lax.Precision.HIGHEST)
    scores = low_back(scores * scaling)
    if allowed is not None:
        scores = jnp.where(allowed[:, None], scores, -1e+30)
    attention_probs = low(jax.nn.softmax(scores, axis=-1))
    mixed_heads = jnp.einsum('bhqk,bkhd->bqhd', attention_probs, split_heads(value_rows), precision=lax.Precision.HIGHEST)
    return mixed_heads.reshape(queries.shape[0], queries.shape[1], -1)

def layer_rows(layer_params, token_values, feature_values, kind_rows):
    attend_triple_matrix, inward_result_matrix, inward_result_offset, inward_center_scale, inward_center_shift, mixing_asker_matrix, visual_lookup_pairs, mixing_result_matrix, mixing_result_offset, mixing_center_scale, mixing_center_shift, widening_matrix, widening_offset, narrowing_matrix, narrowing_offset, perceptron_center_scale, perceptron_center_shift = layer_params
    allowed = kind_rows[:, :, None] == kind_rows[:, None, :]
    model_width = token_values.shape[-1]
    qkv_rows = low(low_back(project(token_values, attend_triple_matrix)))
    mixed_heads = low(low_back(attend(qkv_rows[..., :model_width], qkv_rows[..., model_width:2 * model_width], qkv_rows[..., 2 * model_width:], allowed)))
    first_branch = low_back(project(mixed_heads, inward_result_matrix) + inward_result_offset)
    inner_rows = layer_norm(token_values + first_branch, inward_center_scale, inward_center_shift)
    head_rows = inner_rows[:, :QUERY]
    asked_rows = low(low_back(project(low(head_rows), mixing_asker_matrix)))
    keyval = low(low_back(project(feature_values, visual_lookup_pairs)))
    seen_rows = low(low_back(attend(asked_rows, keyval[..., :model_width], keyval[..., model_width:], None)))
    second_branch = low_back(project(seen_rows, mixing_result_matrix) + mixing_result_offset)
    merged = jnp.concatenate([layer_norm(head_rows + second_branch, mixing_center_scale, mixing_center_shift), inner_rows[:, QUERY:]], axis=1)
    pre_act = low_back(project(low(merged), widening_matrix) + widening_offset)
    activated = low(jax.nn.gelu(pre_act, approximate=False))
    third_branch = low_back(project(activated, narrowing_matrix) + narrowing_offset)
    return layer_norm(merged + third_branch, perceptron_center_scale, perceptron_center_shift)

def contrast(similar, reverse_sims, temper, positive, caption_total):
    image_side = jax.nn.logsumexp(similar / temper, axis=-1)
    text_side = jax.nn.logsumexp(reverse_sims / temper, axis=-1)
    matched = lax.optimization_barrier(jnp.sum(similar * positive, axis=-1)) / temper
    return jnp.sum(image_side + text_side - 2.0 * matched) / (2.0 * caption_total)

def head_loss(finishing_lines, picker, sentence_picture_owner, head_params, temper):
    picture_mapping_matrix, picture_vector_offset, sentence_mapping_matrix, sentence_vector_offset = head_params
    pooled = low(lax.optimization_barrier(jnp.mean(finishing_lines[:, :QUERY], axis=1)))
    image_unit = low(unit_rows(low_back(project(pooled, picture_mapping_matrix) + picture_vector_offset)))
    captions = lax.optimization_barrier(jnp.sum(picker[:, :, :, None] * finishing_lines[:, None, QUERY:, :], axis=2))
    caption_low = low(captions.reshape(-1, captions.shape[-1]))
    text_unit = low(unit_rows(low_back(project(caption_low, sentence_mapping_matrix) + sentence_vector_offset)))
    similar = low_back(jnp.matmul(text_unit, image_unit.T, precision=lax.Precision.HIGHEST))
    chosen = jnp.take(image_unit, sentence_picture_owner, axis=0)
    reverse_sims = low_back(jnp.matmul(chosen, text_unit.T, precision=lax.Precision.HIGHEST))
    image_ids = jnp.arange(IMAGES, dtype=jnp.int32)
    positive = (sentence_picture_owner[:, None] == image_ids[None, :]).astype(jnp.float32)
    return contrast(similar, reverse_sims, temper, positive, CAPTIONS)

def reference(sequence_entries, picture_descriptors, sentence_numbering, sentence_picture_owner, upstream_adjoint, attend_triple_matrix, inward_result_matrix, inward_result_offset, inward_center_scale, inward_center_shift, mixing_asker_matrix, visual_lookup_pairs, mixing_result_matrix, mixing_result_offset, mixing_center_scale, mixing_center_shift, widening_matrix, widening_offset, narrowing_matrix, narrowing_offset, perceptron_center_scale, perceptron_center_shift, picture_mapping_matrix, picture_vector_offset, sentence_mapping_matrix, sentence_vector_offset, logit_sharpness):
    blocks = N_REP * N_FSDP // 8
    layer_inputs = (attend_triple_matrix, inward_result_matrix, inward_result_offset, inward_center_scale, inward_center_shift, mixing_asker_matrix, visual_lookup_pairs, mixing_result_matrix, mixing_result_offset, mixing_center_scale, mixing_center_shift, widening_matrix, widening_offset, narrowing_matrix, narrowing_offset, perceptron_center_scale, perceptron_center_shift)
    block_forward_tuple = tuple((weight.astype(jnp.float32) for weight in layer_inputs))
    loss_forward_tuple = tuple((weight.astype(jnp.float32) for weight in (picture_mapping_matrix, picture_vector_offset, sentence_mapping_matrix, sentence_vector_offset)))
    kinds_all = token_kinds(sentence_numbering)
    picker = caption_picker(sentence_numbering)

    def whole_transformer_block(token_values, layer_params, head_params, temper):

        def block_step(carried, block_rows):
            token_block, feature_block, kind_block = block_rows
            return (carried, layer_rows(layer_params, token_block, feature_block.astype(jnp.float32), kind_block))
        stacked = (token_values.reshape(blocks, -1, ROW_LEN, D), picture_descriptors.reshape(blocks, -1, PATCHES, VIS), kinds_all.reshape(blocks, -1, ROW_LEN))
        _, outputs = lax.scan(jax.checkpoint(block_step), jnp.zeros((), jnp.float32), stacked)
        finishing_lines = outputs.reshape(ROWS, ROW_LEN, D)
        return (finishing_lines, head_loss(finishing_lines, picker, sentence_picture_owner, head_params, temper))
    (finishing_lines, matching_loss_block), reverse_sweep_rule = jax.vjp(whole_transformer_block, sequence_entries.astype(jnp.float32), block_forward_tuple, loss_forward_tuple, logit_sharpness)
    incoming_sequence_adjoint, block_adjoint_tuple, loss_adjoint_tuple, sharpness_adjoint = reverse_sweep_rule((upstream_adjoint.astype(jnp.float32), jnp.ones((), jnp.float32)))
    return (finishing_lines.astype(jnp.bfloat16), incoming_sequence_adjoint, block_adjoint_tuple[0], block_adjoint_tuple[1], block_adjoint_tuple[2], block_adjoint_tuple[3], block_adjoint_tuple[4], block_adjoint_tuple[5], block_adjoint_tuple[6], block_adjoint_tuple[7], block_adjoint_tuple[8], block_adjoint_tuple[9], block_adjoint_tuple[10], block_adjoint_tuple[11], block_adjoint_tuple[12], block_adjoint_tuple[13], block_adjoint_tuple[14], block_adjoint_tuple[15], block_adjoint_tuple[16], loss_adjoint_tuple[0], loss_adjoint_tuple[1], loss_adjoint_tuple[2], loss_adjoint_tuple[3], sharpness_adjoint)
```

```python
from functools import partial

import jax
import jax.numpy as jnp
from jax import lax
from jax.sharding import PartitionSpec as P

HEADS = 12
HEAD = 64
QUERY = 32
CAPS_ROW = 2


def project(values, matrix):
    return jnp.einsum("...d,df->...f", values, matrix, preferred_element_type=jnp.float32)


def project_back(gradient, matrix):
    return jnp.einsum("...f,df->...d", gradient, matrix, preferred_element_type=jnp.float32)


def outer_sum(values, gradient):
    flat_values = values.reshape(-1, values.shape[-1])
    flat_gradient = gradient.reshape(-1, gradient.shape[-1])
    return lax.dot_general(
        flat_values, flat_gradient, (((0,), (0,)), ((), ())), preferred_element_type=jnp.float32
    )


def column_sum(gradient):
    return jnp.sum(gradient.reshape(-1, gradient.shape[-1]), axis=0, dtype=jnp.float32)


def layer_norm(summed, norm_gain, norm_shift):
    center = summed - jnp.mean(summed, axis=-1, keepdims=True)
    spread = jnp.mean(center * center, axis=-1, keepdims=True)
    return center * lax.rsqrt(spread + 1e-06) * norm_gain + norm_shift


def norm_back(summed, norm_gain, norm_shift, gradient):
    _, reverse_sweep_rule = jax.vjp(layer_norm, summed, norm_gain, norm_shift)
    return reverse_sweep_rule(gradient)


def unit_rows(values):
    return values * lax.rsqrt(jnp.sum(values * values, axis=-1, keepdims=True) + 1e-06)


def exact_gelu(values):
    return jax.nn.gelu(values, approximate=False)


def token_kinds(sentence_numbering):
    query_kinds = jnp.zeros((sentence_numbering.shape[0], QUERY), jnp.int32)
    return jnp.concatenate([query_kinds, sentence_numbering + 1], axis=1)


def caption_picker(sentence_numbering):
    caption_ids = jnp.arange(CAPS_ROW, dtype=jnp.int32)
    starts = jnp.sum(
        (sentence_numbering[:, None, :] < caption_ids[None, :, None]).astype(jnp.int32), axis=2
    )
    places = jnp.arange(sentence_numbering.shape[1], dtype=jnp.int32)
    return (places[None, None, :] == starts[:, :, None]).astype(jnp.float32)


def split_heads(values):
    return values.reshape(values.shape[0], values.shape[1], HEADS, values.shape[2] // HEADS)


def scores_of(queries, key_rows, allowed):
    scaling = HEAD ** (-0.5)
    scores = (
        jnp.einsum(
            "bqhd,bkhd->bhqk",
            split_heads(queries),
            split_heads(key_rows),
            preferred_element_type=jnp.float32,
        )
        * scaling
    )
    if allowed is not None:
        scores = jnp.where(allowed[:, None], scores, -1e30)
    return (scores, scaling)


def swap(values, axis, step):
    count = lax.axis_size(axis)
    return lax.ppermute(values, axis, [(i, i ^ step) for i in range(count)])


def bit_of(axis, step):
    return (lax.axis_index(axis) // step) % 2


def bits(axis):
    count = lax.axis_size(axis)
    assert count & (count - 1) == 0
    return [1 << k for k in range(count.bit_length() - 1)]


def route(first):
    rep = [("rep", step) for step in bits("rep")[1:]]
    fsdp = [("fsdp", step) for step in bits("fsdp")]
    return rep + fsdp if first == "rep" else fsdp[:1] + rep + fsdp[1:]


def shard_sum(values, gradient, first):
    flat_values = values.reshape(-1, values.shape[-1])
    flat_gradient = gradient.reshape(-1, gradient.shape[-1])
    half = flat_gradient.shape[1] // 2
    core = bit_of("rep", 1)
    other = lax.dynamic_slice_in_dim(flat_gradient, (1 - core) * half, half, 1)
    mine = lax.dynamic_slice_in_dim(flat_gradient, core * half, half, 1)
    sent = outer_sum(flat_values, other).astype(jnp.bfloat16)
    kept = outer_sum(flat_values, mine).astype(jnp.bfloat16)
    return halves(sent, kept, first)


def halves(sent, kept, first):
    total = add(kept, swap(sent, "rep", 1))
    fsdp = [("fsdp", step) for step in reversed(bits("fsdp"))]
    rep = [("rep", step) for step in reversed(bits("rep")[1:])]
    places = fsdp + rep
    rows = total.shape[0] // 2 ** len(places)
    total = total.reshape((2,) * len(places) + (rows, total.shape[1]))
    for axis, step in route(first):
        at = places.index((axis, step))
        here = bit_of(axis, step)
        away = lax.dynamic_index_in_dim(total, 1 - here, at, False)
        stay = lax.dynamic_index_in_dim(total, here, at, False)
        total = add(stay, swap(away, axis, step))
        places = places[:at] + places[at + 1 :]
    return total


def add(left, right):
    return (left.astype(jnp.float32) + right.astype(jnp.float32)).astype(jnp.bfloat16)


def whole_shard(piece):
    every = lax.all_gather(piece, "rep", axis=0, tiled=False)
    rows, columns = piece.shape
    every = every.reshape(-1, 2, rows, columns).transpose(0, 2, 1, 3)
    return every.reshape(-1, 2 * columns).astype(jnp.float32)


def gather_rows(shard):
    part = shard.shape[0] // lax.axis_size("rep")
    mine = lax.dynamic_slice_in_dim(shard, lax.axis_index("rep") * part, part, 0)
    return lax.all_gather(mine, ("fsdp", "rep"), axis=0, tiled=True)


def gather_columns(shard):
    count = lax.axis_size("rep")
    part = shard.shape[1] // count
    mine = lax.dynamic_slice_in_dim(shard, lax.axis_index("rep") * part, part, 1)
    whole = lax.all_gather(mine, ("rep", "fsdp"), axis=0, tiled=True)
    return whole.reshape(count, -1, part)


def attend(queries, key_rows, value_rows, allowed):
    scores, _ = scores_of(queries, key_rows, allowed)
    highest = jnp.max(scores, axis=-1, keepdims=True)
    exponent = jnp.exp(scores - highest)
    normalizer = jnp.sum(exponent, axis=-1, keepdims=True)
    probs = exponent / normalizer
    mixed_heads = jnp.einsum(
        "bhqk,bkhd->bqhd",
        probs.astype(jnp.bfloat16),
        split_heads(value_rows),
        preferred_element_type=jnp.float32,
    )
    mixed_heads = mixed_heads.reshape(queries.shape[0], queries.shape[1], -1).astype(jnp.bfloat16)
    return (mixed_heads, probs)


def attend_back(queries, key_rows, value_rows, attention_probs, grad_mixed):
    scaling = HEAD ** (-0.5)
    upstream = split_heads(grad_mixed)
    grad_value = jnp.einsum(
        "bhqk,bqhd->bkhd",
        attention_probs.astype(jnp.bfloat16),
        upstream,
        preferred_element_type=jnp.float32,
    )
    grad_probs = jnp.einsum(
        "bqhd,bkhd->bhqk", upstream, split_heads(value_rows), preferred_element_type=jnp.float32
    )
    grad_scores = attention_probs * (
        grad_probs - jnp.sum(attention_probs * grad_probs, axis=-1, keepdims=True)
    )
    grad_scores = grad_scores.astype(jnp.bfloat16)
    grad_query = (
        jnp.einsum(
            "bhqk,bkhd->bqhd",
            grad_scores,
            split_heads(key_rows),
            preferred_element_type=jnp.float32,
        )
        * scaling
    )
    grad_key = (
        jnp.einsum(
            "bhqk,bqhd->bkhd", grad_scores, split_heads(queries), preferred_element_type=jnp.float32
        )
        * scaling
    )
    batch = queries.shape[0]
    return (
        grad_query.reshape(batch, queries.shape[1], -1),
        grad_key.reshape(batch, key_rows.shape[1], -1),
        grad_value.reshape(batch, key_rows.shape[1], -1),
    )


def contrast(similar, reverse_sims, temper, positive, caption_total):
    image_side = jax.nn.logsumexp(similar / temper, axis=-1)
    text_side = jax.nn.logsumexp(reverse_sims / temper, axis=-1)
    matched = jnp.sum(similar * positive, axis=-1) / temper
    return jnp.sum(image_side + text_side - 2.0 * matched) / (2.0 * caption_total)


def on_device(
    sequence_entries,
    picture_descriptors,
    sentence_numbering,
    sentence_picture_owner,
    upstream_adjoint,
    attend_triple_matrix,
    inward_result_matrix,
    inward_result_offset,
    inward_center_scale,
    inward_center_shift,
    mixing_asker_matrix,
    visual_lookup_pairs,
    mixing_result_matrix,
    mixing_result_offset,
    mixing_center_scale,
    mixing_center_shift,
    widening_matrix,
    widening_offset,
    narrowing_matrix,
    narrowing_offset,
    perceptron_center_scale,
    perceptron_center_shift,
    picture_mapping_matrix,
    picture_vector_offset,
    sentence_mapping_matrix,
    sentence_vector_offset,
    logit_sharpness,
):
    f32 = jnp.float32
    bf16 = jnp.bfloat16
    everywhere = ("rep", "fsdp")
    rows, row_len, width = sequence_entries.shape
    segment_of = token_kinds(sentence_numbering)
    allowed = segment_of[:, :, None] == segment_of[:, None, :]
    picker = caption_picker(sentence_numbering)

    vectors = (
        inward_result_offset,
        inward_center_scale,
        inward_center_shift,
        mixing_result_offset,
        mixing_center_scale,
        mixing_center_shift,
        widening_offset,
        narrowing_offset,
        perceptron_center_scale,
        perceptron_center_shift,
        picture_vector_offset,
        sentence_vector_offset,
    )
    packed = lax.all_gather(jnp.concatenate(vectors), "fsdp", axis=0, tiled=False)
    spread = []
    offset = 0
    for vector in vectors:
        size = vector.shape[0]
        spread.append(packed[:, offset : offset + size].reshape(-1).astype(f32))
        offset += size
    (
        self_offset,
        self_scale,
        self_shift,
        cross_offset,
        cross_scale,
        cross_shift,
        wide_offset,
        narrow_offset,
        feed_scale,
        feed_shift,
        image_shift,
        text_shift,
    ) = spread
    owners = lax.all_gather(sentence_picture_owner, everywhere, axis=0, tiled=True)

    w_qkv = gather_rows(attend_triple_matrix)
    w_self_out = gather_rows(inward_result_matrix)
    w_keyval = gather_columns(visual_lookup_pairs)
    w_asker = gather_rows(mixing_asker_matrix)
    w_cross_out = gather_rows(mixing_result_matrix)
    w_up = gather_rows(widening_matrix)
    w_down = gather_rows(narrowing_matrix)
    w_ends = gather_rows(jnp.concatenate([picture_mapping_matrix, sentence_mapping_matrix], axis=1))
    emb = picture_mapping_matrix.shape[1]
    w_image = w_ends[:, :emb]
    w_text = w_ends[:, emb:]

    qkv = project(sequence_entries, w_qkv).astype(bf16)
    q_self, k_self, v_self = (qkv[..., i * width : (i + 1) * width] for i in range(3))
    self_mix, self_probs = attend(q_self, k_self, v_self, allowed)
    first_sum = sequence_entries.astype(f32) + project(self_mix, w_self_out) + self_offset
    inner = layer_norm(first_sum, self_scale, self_shift)

    head_rows = inner[:, :QUERY]
    head_low = head_rows.astype(bf16)
    asked = project(head_low, w_asker).astype(bf16)
    parts = w_keyval.shape[0]
    keyval = jnp.concatenate(
        [project(picture_descriptors, w_keyval[i]).astype(bf16) for i in range(parts)], axis=-1
    )
    k_cross, v_cross = keyval[..., :width], keyval[..., width:]
    cross_mix, cross_probs = attend(asked, k_cross, v_cross, None)
    second_sum = head_rows + project(cross_mix, w_cross_out) + cross_offset
    normed = layer_norm(second_sum, cross_scale, cross_shift)
    merged = jnp.concatenate([normed, inner[:, QUERY:]], axis=1)

    merged_low = merged.astype(bf16)
    pre_act = project(merged_low, w_up) + wide_offset
    activated = exact_gelu(pre_act).astype(bf16)
    third_sum = merged + project(activated, w_down) + narrow_offset
    final = layer_norm(third_sum, feed_scale, feed_shift)
    out = final.astype(bf16)

    pooled_low = jnp.mean(final[:, :QUERY], axis=1).astype(bf16)
    image_raw = project(pooled_low, w_image) + image_shift
    image_unit = unit_rows(image_raw).astype(bf16)
    caption_low = jnp.einsum(
        "rcp,rpd->rcd", picker.astype(bf16), out[:, QUERY:], preferred_element_type=f32
    )
    caption_low = caption_low.astype(bf16).reshape(-1, width)
    text_raw = project(caption_low, w_text) + text_shift
    text_unit = unit_rows(text_raw).astype(bf16)
    units = lax.all_gather(
        jnp.concatenate([image_unit, text_unit], axis=0), everywhere, axis=0, tiled=False
    )
    all_images = units[:, :rows].reshape(-1, emb)
    all_texts = units[:, rows:].reshape(-1, emb)
    image_total = all_images.shape[0]
    text_total = all_texts.shape[0]
    positive = owners[:, None] == jnp.arange(image_total, dtype=jnp.int32)[None, :]
    similar = lax.dot_general(
        all_texts, all_images, (((1,), (1,)), ((), ())), preferred_element_type=f32
    )
    chosen = jnp.dot(positive.astype(bf16), all_images, preferred_element_type=f32).astype(bf16)
    reverse_sims = lax.dot_general(
        chosen, all_texts, (((1,), (1,)), ((), ())), preferred_element_type=f32
    )
    _, contrast_pull = jax.vjp(
        partial(contrast, positive=positive.astype(f32), caption_total=text_total),
        similar,
        reverse_sims,
        logit_sharpness,
    )
    grad_sims, grad_back, sharpness_adjoint = contrast_pull(jnp.ones((), f32))
    grad_sims = grad_sims.astype(bf16)
    grad_back = grad_back.astype(bf16)
    device = lax.axis_index("rep") * lax.axis_size("fsdp") + lax.axis_index("fsdp")
    texts_here = text_unit.shape[0]
    grad_chosen = jnp.dot(grad_back, all_texts, preferred_element_type=f32)
    own_images = device * rows + jnp.arange(rows, dtype=jnp.int32)
    own_positive = (owners[:, None] == own_images[None, :]).astype(f32)
    own_columns = lax.dynamic_slice_in_dim(grad_sims, device * rows, rows, 1)
    grad_image_unit = outer_sum(own_columns, all_texts) + lax.dot_general(
        own_positive,
        grad_chosen,
        (((0,), (0,)), ((), ())),
        precision=lax.Precision.HIGHEST,
        preferred_element_type=f32,
    )
    own_rows = lax.dynamic_slice_in_dim(grad_sims, device * texts_here, texts_here, 0)
    own_back = lax.dynamic_slice_in_dim(grad_back, device * texts_here, texts_here, 1)
    grad_text_unit = jnp.dot(own_rows, all_images, preferred_element_type=f32) + outer_sum(
        own_back, chosen
    )
    _, image_pull = jax.vjp(unit_rows, image_raw)
    grad_image_raw = image_pull(grad_image_unit)[0].astype(bf16)
    _, text_pull = jax.vjp(unit_rows, text_raw)
    grad_text_raw = text_pull(grad_text_unit)[0].astype(bf16)
    grad_pooled = project_back(grad_image_raw, w_image) / QUERY
    grad_captions = project_back(grad_text_raw, w_text).reshape(rows, CAPS_ROW, width)
    grad_caption_rows = jnp.sum(picker[:, :, :, None] * grad_captions[:, :, None, :], axis=1)
    grad_query_rows = jnp.broadcast_to(grad_pooled[:, None, :], (rows, QUERY, width))
    grad_final = upstream_adjoint.astype(f32) + jnp.concatenate(
        [grad_query_rows, grad_caption_rows], axis=1
    )

    grad_third_sum, feed_gain, feed_shift_grad = norm_back(
        third_sum, feed_scale, feed_shift, grad_final
    )
    grad_third = grad_third_sum.astype(bf16)
    down_piece = shard_sum(activated, grad_third, "fsdp")
    grad_active = project_back(grad_third, w_down)
    _, gelu_pull = jax.vjp(exact_gelu, pre_act)
    grad_pre = gelu_pull(grad_active)[0].astype(bf16)
    up_piece = shard_sum(merged_low, grad_pre, "rep")
    grad_merged = grad_third_sum + project_back(grad_pre, w_up)
    ends = jnp.concatenate(
        [outer_sum(pooled_low, grad_image_raw), outer_sum(caption_low, grad_text_raw)], axis=1
    ).astype(bf16)
    core = bit_of("rep", 1)
    ends_sent = lax.dynamic_slice_in_dim(ends, (1 - core) * emb, emb, 1)
    ends_kept = lax.dynamic_slice_in_dim(ends, core * emb, emb, 1)
    ends_piece = halves(ends_sent, ends_kept, "fsdp")

    grad_second_sum, cross_gain, cross_shift_grad = norm_back(
        second_sum, cross_scale, cross_shift, grad_merged[:, :QUERY]
    )
    grad_second = grad_second_sum.astype(bf16)
    grad_cross_mix = project_back(grad_second, w_cross_out).astype(bf16)
    cross_out_piece = shard_sum(cross_mix, grad_second, "fsdp")
    grad_asked, grad_key, grad_value = attend_back(
        asked, k_cross, v_cross, cross_probs, grad_cross_mix
    )
    grad_asked = grad_asked.astype(bf16)
    grad_keyval = jnp.concatenate([grad_key, grad_value], axis=-1).astype(bf16)
    keyval_piece = shard_sum(picture_descriptors, grad_keyval, "rep")
    asker_piece = shard_sum(head_low, grad_asked, "fsdp")
    grad_head = grad_second_sum + project_back(grad_asked, w_asker)
    grad_inner = jnp.concatenate([grad_head, grad_merged[:, QUERY:]], axis=1)

    grad_first_sum, self_gain, self_shift_grad = norm_back(
        first_sum, self_scale, self_shift, grad_inner
    )
    grad_first = grad_first_sum.astype(bf16)
    self_out_piece = shard_sum(self_mix, grad_first, "rep")
    grad_self_mix = project_back(grad_first, w_self_out).astype(bf16)
    grad_q, grad_k, grad_v = attend_back(q_self, k_self, v_self, self_probs, grad_self_mix)
    grad_qkv = jnp.concatenate([grad_q, grad_k, grad_v], axis=-1).astype(bf16)
    qkv_piece = shard_sum(sequence_entries, grad_qkv, "fsdp")
    incoming = grad_first_sum + project_back(grad_qkv, w_qkv)

    early = (
        column_sum(grad_pre),
        column_sum(grad_third),
        feed_gain,
        feed_shift_grad,
        column_sum(grad_second),
        cross_gain,
        cross_shift_grad,
        column_sum(grad_image_raw),
        column_sum(grad_text_raw),
    )
    late = (column_sum(grad_first), self_gain, self_shift_grad)
    shards = []
    for group in (early, late):
        summed = lax.psum(jnp.concatenate(group), everywhere)
        offset = 0
        for vector in group:
            size = vector.shape[0]
            share = size // lax.axis_size("fsdp")
            start = offset + lax.axis_index("fsdp") * share
            shards.append(lax.dynamic_slice_in_dim(summed, start, share, 0))
            offset += size
    (
        up_bias,
        down_bias,
        feed_gain,
        feed_shift_grad,
        cross_bias,
        cross_gain,
        cross_shift_grad,
        image_bias,
        text_bias,
        self_bias,
        self_gain,
        self_shift_grad,
    ) = shards
    ends_shard = whole_shard(ends_piece)
    return (
        out,
        incoming,
        whole_shard(qkv_piece),
        whole_shard(self_out_piece),
        self_bias,
        self_gain,
        self_shift_grad,
        whole_shard(asker_piece),
        whole_shard(keyval_piece),
        whole_shard(cross_out_piece),
        cross_bias,
        cross_gain,
        cross_shift_grad,
        whole_shard(up_piece),
        up_bias,
        whole_shard(down_piece),
        down_bias,
        feed_gain,
        feed_shift_grad,
        ends_shard[:, :emb],
        image_bias,
        ends_shard[:, emb:],
        text_bias,
        sharpness_adjoint,
    )


def solution(mesh):
    placed = (
        P(("rep", "fsdp"), None, None),
        P(("rep", "fsdp"), None, None),
        P(("rep", "fsdp"), None),
        P(("rep", "fsdp")),
        P(("rep", "fsdp"), None, None),
        P("fsdp", None),
        P("fsdp", None),
        P("fsdp"),
        P("fsdp"),
        P("fsdp"),
        P("fsdp", None),
        P("fsdp", None),
        P("fsdp", None),
        P("fsdp"),
        P("fsdp"),
        P("fsdp"),
        P("fsdp", None),
        P("fsdp"),
        P("fsdp", None),
        P("fsdp"),
        P("fsdp"),
        P("fsdp"),
        P("fsdp", None),
        P("fsdp"),
        P("fsdp", None),
        P("fsdp"),
        P(),
    )
    return jax.shard_map(
        on_device,
        mesh=mesh,
        in_specs=placed,
        out_specs=(
            P(("rep", "fsdp"), None, None),
            P(("rep", "fsdp"), None, None),
            P("fsdp", None),
            P("fsdp", None),
            P("fsdp"),
            P("fsdp"),
            P("fsdp"),
            P("fsdp", None),
            P("fsdp", None),
            P("fsdp", None),
            P("fsdp"),
            P("fsdp"),
            P("fsdp"),
            P("fsdp", None),
            P("fsdp"),
            P("fsdp", None),
            P("fsdp"),
            P("fsdp"),
            P("fsdp"),
            P("fsdp", None),
            P("fsdp"),
            P("fsdp", None),
            P("fsdp"),
            P(),
        ),
        check_vma=False,
    )
```

```python
from functools import partial

import jax
import jax.numpy as jnp
from jax import lax
from jax.sharding import PartitionSpec as P

HEADS = 12
HEAD = 64
QUERY = 32
CAPS_ROW = 2


def project(values, matrix):
    return jnp.einsum("...d,df->...f", values, matrix, preferred_element_type=jnp.float32)


def project_back(gradient, matrix):
    return jnp.einsum("...f,df->...d", gradient, matrix, preferred_element_type=jnp.float32)


def outer_sum(values, gradient):
    flat_values = values.reshape(-1, values.shape[-1])
    flat_gradient = gradient.reshape(-1, gradient.shape[-1])
    return lax.dot_general(
        flat_values, flat_gradient, (((0,), (0,)), ((), ())), preferred_element_type=jnp.float32
    )


def column_sum(gradient):
    return jnp.sum(gradient.reshape(-1, gradient.shape[-1]), axis=0, dtype=jnp.float32)


def layer_norm(summed, norm_gain, norm_shift):
    center = summed - jnp.mean(summed, axis=-1, keepdims=True)
    spread = jnp.mean(center * center, axis=-1, keepdims=True)
    return center * lax.rsqrt(spread + 1e-06) * norm_gain + norm_shift


def norm_back(summed, norm_gain, norm_shift, gradient):
    _, reverse_sweep_rule = jax.vjp(layer_norm, summed, norm_gain, norm_shift)
    return reverse_sweep_rule(gradient)


def unit_rows(values):
    return values * lax.rsqrt(jnp.sum(values * values, axis=-1, keepdims=True) + 1e-06)


def exact_gelu(values):
    return jax.nn.gelu(values, approximate=False)


def token_kinds(sentence_numbering):
    query_kinds = jnp.zeros((sentence_numbering.shape[0], QUERY), jnp.int32)
    return jnp.concatenate([query_kinds, sentence_numbering + 1], axis=1)


def caption_picker(sentence_numbering):
    caption_ids = jnp.arange(CAPS_ROW, dtype=jnp.int32)
    starts = jnp.sum(
        (sentence_numbering[:, None, :] < caption_ids[None, :, None]).astype(jnp.int32), axis=2
    )
    places = jnp.arange(sentence_numbering.shape[1], dtype=jnp.int32)
    return (places[None, None, :] == starts[:, :, None]).astype(jnp.float32)


def split_heads(values):
    return values.reshape(values.shape[0], values.shape[1], HEADS, values.shape[2] // HEADS)


def scores_of(queries, key_rows, allowed):
    scaling = HEAD ** (-0.5)
    scores = (
        jnp.einsum(
            "bqhd,bkhd->bhqk",
            split_heads(queries),
            split_heads(key_rows),
            preferred_element_type=jnp.float32,
        )
        * scaling
    )
    if allowed is not None:
        scores = jnp.where(allowed[:, None], scores, -1e30)
    return (scores, scaling)


def swap(values, axis, step):
    count = lax.axis_size(axis)
    return lax.ppermute(values, axis, [(i, i ^ step) for i in range(count)])


def bit_of(axis, step):
    return (lax.axis_index(axis) // step) % 2


def bits(axis):
    count = lax.axis_size(axis)
    assert count & (count - 1) == 0
    return [1 << k for k in range(count.bit_length() - 1)]


def route(first):
    rep = [("rep", step) for step in bits("rep")[1:]]
    fsdp = [("fsdp", step) for step in bits("fsdp")]
    return rep + fsdp if first == "rep" else fsdp[:1] + rep + fsdp[1:]


def add(left, right):
    return (left.astype(jnp.float32) + right.astype(jnp.float32)).astype(jnp.bfloat16)


class Flow:
    def __init__(self, sent, kept, first):
        self.kept = kept
        self.got = swap(sent, "rep", 1)
        self.left = route(first)
        fsdp = [("fsdp", step) for step in reversed(bits("fsdp"))]
        rep = [("rep", step) for step in reversed(bits("rep")[1:])]
        self.places = fsdp + rep
        rows = kept.shape[0] // 2 ** len(self.places)
        self.shape = (2,) * len(self.places) + (rows, kept.shape[1])

    def advance(self):
        if self.got is None:
            return
        total = add(self.kept, self.got)
        if self.shape is not None:
            total = total.reshape(self.shape)
            self.shape = None
        self.kept, self.got = total, None
        if self.left:
            (axis, step), self.left = self.left[0], self.left[1:]
            at = self.places.index((axis, step))
            self.places = self.places[:at] + self.places[at + 1 :]
            here = bit_of(axis, step)
            away = lax.dynamic_index_in_dim(total, 1 - here, at, False)
            self.kept = lax.dynamic_index_in_dim(total, here, at, False)
            self.got = swap(away, axis, step)

    def shard(self):
        whole = self.kept
        for step in bits("rep")[1:]:
            whole = join(whole, 0, "rep", step)
        whole = whole.reshape(-1, whole.shape[-1])
        return join(whole, 1, "rep", 1).reshape(whole.shape[0], -1).astype(jnp.float32)


def tie(value, *flows):
    flows = [flow for flow in flows if flow.got is not None]
    tied = lax.optimization_barrier((value, *[flow.got for flow in flows]))
    for flow, got in zip(flows, tied[1:]):
        flow.got = got
        flow.advance()
    return tied[0]


def gradient_halves(values, gradient):
    flat_values = values.reshape(-1, values.shape[-1])
    flat_gradient = gradient.reshape(-1, gradient.shape[-1])
    half = flat_gradient.shape[1] // 2
    core = bit_of("rep", 1)
    other = lax.dynamic_slice_in_dim(flat_gradient, (1 - core) * half, half, 1)
    mine = lax.dynamic_slice_in_dim(flat_gradient, core * half, half, 1)
    return (
        outer_sum(flat_values, other).astype(jnp.bfloat16),
        outer_sum(flat_values, mine).astype(jnp.bfloat16),
    )


def blocks_of(shard, widths):
    half = shard.shape[1] // 2
    blocks = []
    start = 0
    for width in widths:
        size = width // 2
        pair = [shard[:, at + start : at + start + size] for at in (0, half)]
        blocks.append(jnp.concatenate(pair, axis=1))
        start += size
    return blocks


def side_by_side(*pairs):
    return tuple(jnp.concatenate(blocks, axis=1) for blocks in zip(*pairs))


def join(values, at, axis, step):
    theirs = swap(values, axis, step)
    first = bit_of(axis, step) == 0
    return jnp.stack([jnp.where(first, values, theirs), jnp.where(first, theirs, values)], axis=at)


def join_fsdp(values):
    for step in bits("fsdp"):
        values = join(values, 0, "fsdp", step)
        values = values.reshape(-1, *values.shape[2:])
    return values


def join_all(values):
    values = join_fsdp(values)
    for step in bits("rep"):
        values = join(values, 0, "rep", step)
        values = values.reshape(-1, *values.shape[2:])
    return values


def sum_everywhere(values):
    for axis in ("rep", "fsdp"):
        for step in bits(axis):
            values = values + swap(values, axis, step)
    return values


def gather_rows(shard):
    part = shard.shape[0] // lax.axis_size("rep")
    mine = lax.dynamic_slice_in_dim(shard, lax.axis_index("rep") * part, part, 0)
    return lax.all_gather(mine, ("fsdp", "rep"), axis=0, tiled=True)


def part_of(shard, count, at, axis):
    size = shard.shape[axis] // count
    return lax.dynamic_slice_in_dim(shard, at * size, size, axis)


def exchange_rows(shard, first):
    count = lax.axis_size("rep")
    mine = part_of(shard, count, lax.axis_index("rep"), 0)
    rows, columns = mine.shape
    whole = mine[None]
    fsdp, rep = bits("fsdp"), bits("rep")
    for step in fsdp[1:]:
        whole = join(whole, 0, "fsdp", step).reshape(-1, rows, columns)
    if first == "rep":
        whole = whole[:, None]
        for step in rep[1:]:
            whole = join(whole, 1, "rep", step).reshape(whole.shape[0], -1, rows, columns)
        whole = join(whole, 1, "fsdp", 1)
    else:
        whole = join(whole, 1, "fsdp", 1)[:, :, None]
        for step in rep[1:]:
            whole = join(whole, 2, "rep", step).reshape(*whole.shape[:2], -1, rows, columns)
    whole = join(whole, 3, "rep", 1)
    return whole.reshape(-1, columns)


def exchange_columns(shard, first):
    fsdp, rep = bits("fsdp"), bits("rep")
    mine = part_of(shard, 2, bit_of("rep", 1), 1)
    mine = part_of(mine, 2 ** len(rep[1:]), lax.axis_index("rep") // 2, 0)
    rows, columns = mine.shape
    whole = mine[None]
    for step in fsdp[1:]:
        whole = join(whole, 0, "fsdp", step).reshape(-1, rows, columns)
    if first == "rep":
        whole = whole[:, None]
        for step in rep[1:]:
            whole = join(whole, 1, "rep", step).reshape(whole.shape[0], -1, rows, columns)
        whole = join(whole, 1, "fsdp", 1)
    else:
        whole = join(whole, 1, "fsdp", 1)[:, :, None]
        for step in rep[1:]:
            whole = join(whole, 2, "rep", step).reshape(*whole.shape[:2], -1, rows, columns)
    whole = whole.reshape(-1, columns)
    theirs = swap(whole, "rep", 1)
    core = bit_of("rep", 1) == 0
    return (jnp.where(core, whole, theirs), jnp.where(core, theirs, whole))


def attend(queries, key_rows, value_rows, allowed):
    scores, _ = scores_of(queries, key_rows, allowed)
    highest = jnp.max(scores, axis=-1, keepdims=True)
    exponent = jnp.exp(scores - highest)
    normalizer = jnp.sum(exponent, axis=-1, keepdims=True)
    probs = exponent / normalizer
    mixed_heads = jnp.einsum(
        "bhqk,bkhd->bqhd",
        probs.astype(jnp.bfloat16),
        split_heads(value_rows),
        preferred_element_type=jnp.float32,
    )
    mixed_heads = mixed_heads.reshape(queries.shape[0], queries.shape[1], -1).astype(jnp.bfloat16)
    return (mixed_heads, probs)


def attend_back(queries, key_rows, value_rows, attention_probs, grad_mixed):
    scaling = HEAD ** (-0.5)
    upstream = split_heads(grad_mixed)
    grad_value = jnp.einsum(
        "bhqk,bqhd->bkhd",
        attention_probs.astype(jnp.bfloat16),
        upstream,
        preferred_element_type=jnp.float32,
    )
    grad_probs = jnp.einsum(
        "bqhd,bkhd->bhqk", upstream, split_heads(value_rows), preferred_element_type=jnp.float32
    )
    grad_scores = attention_probs * (
        grad_probs - jnp.sum(attention_probs * grad_probs, axis=-1, keepdims=True)
    )
    grad_scores = grad_scores.astype(jnp.bfloat16)
    grad_query = (
        jnp.einsum(
            "bhqk,bkhd->bqhd",
            grad_scores,
            split_heads(key_rows),
            preferred_element_type=jnp.float32,
        )
        * scaling
    )
    grad_key = (
        jnp.einsum(
            "bhqk,bqhd->bkhd", grad_scores, split_heads(queries), preferred_element_type=jnp.float32
        )
        * scaling
    )
    batch = queries.shape[0]
    return (
        grad_query.reshape(batch, queries.shape[1], -1),
        grad_key.reshape(batch, key_rows.shape[1], -1),
        grad_value.reshape(batch, key_rows.shape[1], -1),
    )


def contrast(similar, reverse_sims, temper, positive, caption_total):
    image_side = jax.nn.logsumexp(similar / temper, axis=-1)
    text_side = jax.nn.logsumexp(reverse_sims / temper, axis=-1)
    matched = jnp.sum(similar * positive, axis=-1) / temper
    return jnp.sum(image_side + text_side - 2.0 * matched) / (2.0 * caption_total)


def on_device(
    sequence_entries,
    picture_descriptors,
    sentence_numbering,
    sentence_picture_owner,
    upstream_adjoint,
    attend_triple_matrix,
    inward_result_matrix,
    inward_result_offset,
    inward_center_scale,
    inward_center_shift,
    mixing_asker_matrix,
    visual_lookup_pairs,
    mixing_result_matrix,
    mixing_result_offset,
    mixing_center_scale,
    mixing_center_shift,
    widening_matrix,
    widening_offset,
    narrowing_matrix,
    narrowing_offset,
    perceptron_center_scale,
    perceptron_center_shift,
    picture_mapping_matrix,
    picture_vector_offset,
    sentence_mapping_matrix,
    sentence_vector_offset,
    logit_sharpness,
):
    f32 = jnp.float32
    bf16 = jnp.bfloat16
    everywhere = ("rep", "fsdp")
    rows, row_len, width = sequence_entries.shape
    segment_of = token_kinds(sentence_numbering)
    allowed = segment_of[:, :, None] == segment_of[:, None, :]
    picker = caption_picker(sentence_numbering)

    vectors = (
        inward_result_offset,
        inward_center_scale,
        inward_center_shift,
        mixing_result_offset,
        mixing_center_scale,
        mixing_center_shift,
        widening_offset,
        narrowing_offset,
        perceptron_center_scale,
        perceptron_center_shift,
        picture_vector_offset,
        sentence_vector_offset,
    )
    packed = join_fsdp(jnp.concatenate(vectors)[None])
    spread = []
    offset = 0
    for vector in vectors:
        size = vector.shape[0]
        spread.append(packed[:, offset : offset + size].reshape(-1).astype(f32))
        offset += size
    (
        self_offset,
        self_scale,
        self_shift,
        cross_offset,
        cross_scale,
        cross_shift,
        wide_offset,
        narrow_offset,
        feed_scale,
        feed_shift,
        image_shift,
        text_shift,
    ) = spread
    owners = join_all(sentence_picture_owner[None]).reshape(-1)

    emb = picture_mapping_matrix.shape[1]
    w_self = gather_rows(jnp.concatenate([attend_triple_matrix, inward_result_matrix], axis=1))
    w_qkv, w_self_out = w_self[:, : 3 * width], w_self[:, 3 * width :]
    w_keys, w_values = exchange_columns(visual_lookup_pairs, "rep")
    w_rest = gather_rows(
        jnp.concatenate(
            [
                mixing_asker_matrix,
                mixing_result_matrix,
                widening_matrix,
                picture_mapping_matrix,
                sentence_mapping_matrix,
            ],
            axis=1,
        )
    )
    w_asker, w_cross_out = w_rest[:, :width], w_rest[:, width : 2 * width]
    w_up = w_rest[:, 2 * width : -2 * emb]
    w_image, w_text = w_rest[:, -2 * emb : -emb], w_rest[:, -emb:]
    w_down = exchange_rows(narrowing_matrix, "fsdp")

    qkv = project(sequence_entries, w_qkv).astype(bf16)
    q_self, k_self, v_self = (qkv[..., i * width : (i + 1) * width] for i in range(3))
    self_mix, self_probs = attend(q_self, k_self, v_self, allowed)
    first_sum = sequence_entries.astype(f32) + project(self_mix, w_self_out) + self_offset
    inner = layer_norm(first_sum, self_scale, self_shift)

    head_rows = inner[:, :QUERY]
    head_low = head_rows.astype(bf16)
    asked = project(head_low, w_asker).astype(bf16)
    k_cross = project(picture_descriptors, w_keys).astype(bf16)
    v_cross = project(picture_descriptors, w_values).astype(bf16)
    cross_mix, cross_probs = attend(asked, k_cross, v_cross, None)
    second_sum = head_rows + project(cross_mix, w_cross_out) + cross_offset
    normed = layer_norm(second_sum, cross_scale, cross_shift)
    merged = jnp.concatenate([normed, inner[:, QUERY:]], axis=1)

    merged_low = merged.astype(bf16)
    pre_act = project(merged_low, w_up) + wide_offset
    activated = exact_gelu(pre_act).astype(bf16)
    third_sum = merged + project(activated, w_down) + narrow_offset
    final = layer_norm(third_sum, feed_scale, feed_shift)
    out = final.astype(bf16)

    pooled_low = jnp.mean(final[:, :QUERY], axis=1).astype(bf16)
    image_raw = project(pooled_low, w_image) + image_shift
    image_unit = unit_rows(image_raw).astype(bf16)
    caption_low = jnp.einsum(
        "rcp,rpd->rcd", picker.astype(bf16), out[:, QUERY:], preferred_element_type=f32
    )
    caption_low = caption_low.astype(bf16).reshape(-1, width)
    text_raw = project(caption_low, w_text) + text_shift
    text_unit = unit_rows(text_raw).astype(bf16)
    units = join_all(jnp.concatenate([image_unit, text_unit], axis=0)[None])
    all_images = units[:, :rows].reshape(-1, emb)
    all_texts = units[:, rows:].reshape(-1, emb)
    image_total = all_images.shape[0]
    text_total = all_texts.shape[0]
    positive = owners[:, None] == jnp.arange(image_total, dtype=jnp.int32)[None, :]
    similar = lax.dot_general(
        all_texts, all_images, (((1,), (1,)), ((), ())), preferred_element_type=f32
    )
    chosen = jnp.dot(positive.astype(bf16), all_images, preferred_element_type=f32).astype(bf16)
    reverse_sims = lax.dot_general(
        chosen, all_texts, (((1,), (1,)), ((), ())), preferred_element_type=f32
    )
    _, contrast_pull = jax.vjp(
        partial(contrast, positive=positive.astype(f32), caption_total=text_total),
        similar,
        reverse_sims,
        logit_sharpness,
    )
    grad_sims, grad_back, sharpness_adjoint = contrast_pull(jnp.ones((), f32))
    grad_sims = grad_sims.astype(bf16)
    grad_back = grad_back.astype(bf16)
    device = lax.axis_index("rep") * lax.axis_size("fsdp") + lax.axis_index("fsdp")
    texts_here = text_unit.shape[0]
    grad_chosen = jnp.dot(grad_back, all_texts, preferred_element_type=f32)
    own_images = device * rows + jnp.arange(rows, dtype=jnp.int32)
    own_positive = (owners[:, None] == own_images[None, :]).astype(f32)
    own_columns = lax.dynamic_slice_in_dim(grad_sims, device * rows, rows, 1)
    grad_image_unit = outer_sum(own_columns, all_texts) + lax.dot_general(
        own_positive,
        grad_chosen,
        (((0,), (0,)), ((), ())),
        precision=lax.Precision.HIGHEST,
        preferred_element_type=f32,
    )
    own_rows = lax.dynamic_slice_in_dim(grad_sims, device * texts_here, texts_here, 0)
    own_back = lax.dynamic_slice_in_dim(grad_back, device * texts_here, texts_here, 1)
    grad_text_unit = jnp.dot(own_rows, all_images, preferred_element_type=f32) + outer_sum(
        own_back, chosen
    )
    _, image_pull = jax.vjp(unit_rows, image_raw)
    grad_image_raw = image_pull(grad_image_unit)[0].astype(bf16)
    _, text_pull = jax.vjp(unit_rows, text_raw)
    grad_text_raw = text_pull(grad_text_unit)[0].astype(bf16)
    grad_pooled = project_back(grad_image_raw, w_image) / QUERY
    grad_captions = project_back(grad_text_raw, w_text).reshape(rows, CAPS_ROW, width)
    grad_caption_rows = jnp.sum(picker[:, :, :, None] * grad_captions[:, :, None, :], axis=1)
    grad_query_rows = jnp.broadcast_to(grad_pooled[:, None, :], (rows, QUERY, width))
    grad_final = upstream_adjoint.astype(f32) + jnp.concatenate(
        [grad_query_rows, grad_caption_rows], axis=1
    )

    grad_third_sum, feed_gain, feed_shift_grad = norm_back(
        third_sum, feed_scale, feed_shift, grad_final
    )
    grad_third = grad_third_sum.astype(bf16)
    down = Flow(*gradient_halves(activated, grad_third), "fsdp")
    grad_active = project_back(grad_third, w_down)
    _, gelu_pull = jax.vjp(exact_gelu, pre_act)
    grad_pre = gelu_pull(grad_active)[0].astype(bf16)
    grad_pre = tie(grad_pre, down)
    ends = jnp.concatenate(
        [outer_sum(pooled_low, grad_image_raw), outer_sum(caption_low, grad_text_raw)], axis=1
    ).astype(bf16)
    ends_halves = (part_of(ends, 2, 1 - bit_of("rep", 1), 1), part_of(ends, 2, bit_of("rep", 1), 1))
    up = Flow(*side_by_side(gradient_halves(merged_low, grad_pre), ends_halves), "rep")
    grad_merged = grad_third_sum + project_back(grad_pre, w_up)
    grad_merged = tie(grad_merged, up)

    grad_second_sum, cross_gain, cross_shift_grad = norm_back(
        second_sum, cross_scale, cross_shift, grad_merged[:, :QUERY]
    )
    grad_second = grad_second_sum.astype(bf16)
    grad_cross_mix = project_back(grad_second, w_cross_out).astype(bf16)
    cross_out_halves = gradient_halves(cross_mix, grad_second)
    grad_asked, grad_key, grad_value = attend_back(
        asked, k_cross, v_cross, cross_probs, grad_cross_mix
    )
    grad_asked = grad_asked.astype(bf16)
    grad_asked = tie(grad_asked, down, up)
    core_zero = bit_of("rep", 1) == 0
    grad_key = grad_key.astype(bf16)
    grad_value = grad_value.astype(bf16)
    keyval = Flow(
        outer_sum(picture_descriptors, jnp.where(core_zero, grad_value, grad_key)).astype(bf16),
        outer_sum(picture_descriptors, jnp.where(core_zero, grad_key, grad_value)).astype(bf16),
        "fsdp",
    )
    asker_halves = gradient_halves(head_low, grad_asked)
    grad_head = grad_second_sum + project_back(grad_asked, w_asker)
    grad_inner = jnp.concatenate([grad_head, grad_merged[:, QUERY:]], axis=1)
    grad_inner = tie(grad_inner, down, keyval)

    grad_first_sum, self_gain, self_shift_grad = norm_back(
        first_sum, self_scale, self_shift, grad_inner
    )
    grad_first = grad_first_sum.astype(bf16)
    middle = Flow(
        *side_by_side(cross_out_halves, asker_halves, gradient_halves(self_mix, grad_first)), "rep"
    )
    grad_self_mix = project_back(grad_first, w_self_out).astype(bf16)
    grad_self_mix = tie(grad_self_mix, up, middle)
    grad_q, grad_k, grad_v = attend_back(q_self, k_self, v_self, self_probs, grad_self_mix)
    grad_qkv = jnp.concatenate([grad_q, grad_k, grad_v], axis=-1).astype(bf16)
    grad_qkv = tie(grad_qkv, down, up, keyval)
    cut = 4 * grad_qkv.shape[-1] // 9
    left = Flow(*gradient_halves(sequence_entries, grad_qkv[..., :cut]), "rep")
    right = Flow(*gradient_halves(sequence_entries, grad_qkv[..., cut:]), "fsdp")
    flows = (down, up, keyval, middle, left, right)
    incoming = grad_first_sum + project_back(grad_qkv, w_qkv)
    while any(flow.got is not None for flow in flows):
        for flow in flows:
            flow.advance()

    early = (
        column_sum(grad_pre),
        column_sum(grad_third),
        feed_gain,
        feed_shift_grad,
        column_sum(grad_second),
        cross_gain,
        cross_shift_grad,
        column_sum(grad_image_raw),
        column_sum(grad_text_raw),
    )
    late = (column_sum(grad_first), self_gain, self_shift_grad)
    shards = []
    for group in (early, late):
        summed = sum_everywhere(jnp.concatenate(group)[None])[0]
        offset = 0
        for vector in group:
            size = vector.shape[0]
            share = size // lax.axis_size("fsdp")
            start = offset + lax.axis_index("fsdp") * share
            shards.append(lax.dynamic_slice_in_dim(summed, start, share, 0))
            offset += size
    (
        up_bias,
        down_bias,
        feed_gain,
        feed_shift_grad,
        cross_bias,
        cross_gain,
        cross_shift_grad,
        image_bias,
        text_bias,
        self_bias,
        self_gain,
        self_shift_grad,
    ) = shards
    up_shard, middle_shard = up.shard(), middle.shard()
    inner_width = up_bias.shape[0] * lax.axis_size("fsdp")
    up_grad, ends_grad = blocks_of(up_shard, (inner_width, 2 * emb))
    cross_out_grad, asker_grad, self_out_grad = blocks_of(middle_shard, (width,) * 3)
    qkv_grad = jnp.concatenate([left.shard(), right.shard()], axis=1)
    return (
        out,
        incoming,
        qkv_grad,
        self_out_grad,
        self_bias,
        self_gain,
        self_shift_grad,
        asker_grad,
        keyval.shard(),
        cross_out_grad,
        cross_bias,
        cross_gain,
        cross_shift_grad,
        up_grad,
        up_bias,
        down.shard(),
        down_bias,
        feed_gain,
        feed_shift_grad,
        ends_grad[:, :emb],
        image_bias,
        ends_grad[:, emb:],
        text_bias,
        sharpness_adjoint,
    )


def solution(mesh):
    placed = (
        P(("rep", "fsdp"), None, None),
        P(("rep", "fsdp"), None, None),
        P(("rep", "fsdp"), None),
        P(("rep", "fsdp")),
        P(("rep", "fsdp"), None, None),
        P("fsdp", None),
        P("fsdp", None),
        P("fsdp"),
        P("fsdp"),
        P("fsdp"),
        P("fsdp", None),
        P("fsdp", None),
        P("fsdp", None),
        P("fsdp"),
        P("fsdp"),
        P("fsdp"),
        P("fsdp", None),
        P("fsdp"),
        P("fsdp", None),
        P("fsdp"),
        P("fsdp"),
        P("fsdp"),
        P("fsdp", None),
        P("fsdp"),
        P("fsdp", None),
        P("fsdp"),
        P(),
    )
    return jax.shard_map(
        on_device,
        mesh=mesh,
        in_specs=placed,
        out_specs=(
            P(("rep", "fsdp"), None, None),
            P(("rep", "fsdp"), None, None),
            P("fsdp", None),
            P("fsdp", None),
            P("fsdp"),
            P("fsdp"),
            P("fsdp"),
            P("fsdp", None),
            P("fsdp", None),
            P("fsdp", None),
            P("fsdp"),
            P("fsdp"),
            P("fsdp"),
            P("fsdp", None),
            P("fsdp"),
            P("fsdp", None),
            P("fsdp"),
            P("fsdp"),
            P("fsdp"),
            P("fsdp", None),
            P("fsdp"),
            P("fsdp", None),
            P("fsdp"),
            P(),
        ),
        check_vma=False,
    )
```

```python
from functools import partial

import jax
import jax.numpy as jnp
from jax import lax
from jax.sharding import PartitionSpec as P

HEADS = 12
HEAD = 64
QUERY = 32
CAPS_ROW = 2


def project(values, matrix):
    return jnp.einsum("...d,df->...f", values, matrix, preferred_element_type=jnp.float32)


def project_back(gradient, matrix):
    return jnp.einsum("...f,df->...d", gradient, matrix, preferred_element_type=jnp.float32)


def outer_sum(values, gradient):
    flat_values = values.reshape(-1, values.shape[-1])
    flat_gradient = gradient.reshape(-1, gradient.shape[-1])
    return lax.dot_general(
        flat_values, flat_gradient, (((0,), (0,)), ((), ())), preferred_element_type=jnp.float32
    )


def column_sum(gradient):
    return jnp.sum(gradient.reshape(-1, gradient.shape[-1]), axis=0, dtype=jnp.float32)


def layer_norm(summed, norm_gain, norm_shift):
    center = summed - jnp.mean(summed, axis=-1, keepdims=True)
    spread = jnp.mean(center * center, axis=-1, keepdims=True)
    return center * lax.rsqrt(spread + 1e-06) * norm_gain + norm_shift


def norm_back(summed, norm_gain, norm_shift, gradient):
    _, reverse_sweep_rule = jax.vjp(layer_norm, summed, norm_gain, norm_shift)
    return reverse_sweep_rule(gradient)


def unit_rows(values):
    return values * lax.rsqrt(jnp.sum(values * values, axis=-1, keepdims=True) + 1e-06)


def exact_gelu(values):
    return jax.nn.gelu(values, approximate=False)


def token_kinds(sentence_numbering):
    query_kinds = jnp.zeros((sentence_numbering.shape[0], QUERY), jnp.int32)
    return jnp.concatenate([query_kinds, sentence_numbering + 1], axis=1)


def caption_picker(sentence_numbering):
    caption_ids = jnp.arange(CAPS_ROW, dtype=jnp.int32)
    starts = jnp.sum(
        (sentence_numbering[:, None, :] < caption_ids[None, :, None]).astype(jnp.int32), axis=2
    )
    places = jnp.arange(sentence_numbering.shape[1], dtype=jnp.int32)
    return (places[None, None, :] == starts[:, :, None]).astype(jnp.float32)


def split_heads(values):
    return values.reshape(values.shape[0], values.shape[1], HEADS, values.shape[2] // HEADS)


def scores_of(queries, key_rows, allowed):
    scaling = HEAD ** (-0.5)
    scores = (
        jnp.einsum(
            "bqhd,bkhd->bhqk",
            split_heads(queries),
            split_heads(key_rows),
            preferred_element_type=jnp.float32,
        )
        * scaling
    )
    if allowed is not None:
        scores = jnp.where(allowed[:, None], scores, -1e30)
    return (scores, scaling)


def swap(values, axis, step):
    count = lax.axis_size(axis)
    return lax.ppermute(values, axis, [(i, i ^ step) for i in range(count)])


def bit_of(axis, step):
    return (lax.axis_index(axis) // step) % 2


def bits(axis):
    count = lax.axis_size(axis)
    assert count & (count - 1) == 0
    return [1 << k for k in range(count.bit_length() - 1)]


def add(left, right):
    return (left.astype(jnp.float32) + right.astype(jnp.float32)).astype(jnp.bfloat16)


class Task:
    def __init__(self, steps):
        self.steps = steps
        self.result = None
        self.got = next(steps)

    def advance(self, got):
        try:
            self.got = self.steps.send(got)
        except StopIteration as end:
            self.got, self.result = None, end.value


def tie(value, *tasks):
    tasks = [task for task in tasks if task.got is not None]
    tied = lax.optimization_barrier((value, *[task.got for task in tasks]))
    for task, got in zip(tasks, tied[1:]):
        task.advance(got)
    return tied[0]


def lockstep(*tasks):
    tasks = [task for task in tasks if task.got is not None]
    tied = lax.optimization_barrier(tuple(task.got for task in tasks))
    for task, got in zip(tasks, tied):
        task.advance(got)


def flow(sent, kept, first):
    got = yield swap(sent, "rep", 1)
    total = add(kept, got)
    fsdp = [("fsdp", step) for step in reversed(bits("fsdp"))]
    rep = [("rep", step) for step in reversed(bits("rep")[1:])]
    places = fsdp + rep
    rows = total.shape[0] // 2 ** len(places)
    total = total.reshape((2,) * len(places) + (rows, total.shape[1]))
    for axis, step in rep + fsdp[-1:] if first == "rep" else fsdp[-1:] + rep:
        total, away = parted(total, places.index((axis, step)), axis, step)
        places.remove((axis, step))
        got = yield swap(away, axis, step)
        total = add(total, got)
    return total


def parted(total, at, axis, step):
    here = bit_of(axis, step)
    away = lax.dynamic_index_in_dim(total, 1 - here, at, False)
    return lax.dynamic_index_in_dim(total, here, at, False), away


def shards(blocks, rows):
    total = jnp.concatenate([laid_out(block, rows) for block in blocks], axis=-1)
    left = list(reversed(bits("fsdp")[1:]))
    for step in bits("fsdp")[1:]:
        total, away = parted(total, left.index(step), "fsdp", step)
        left.remove(step)
        got = yield swap(away, "fsdp", step)
        total = add(total, got)
    total = total[None]
    for step in bits("rep")[1:]:
        total = yield from joined(total, 0, "rep", step)
        total = total.reshape(-1, *total.shape[2:])
    total = yield from joined(total, 2, "rep", 1)
    chips = total.shape[0]
    results = []
    start = 0
    for block in blocks:
        height, columns = block.shape[-2:]
        count = -(-height // rows)
        part = total[..., start : start + count * columns].astype(jnp.float32)
        start += count * columns
        part = part.reshape(chips, rows, 2, count, columns).transpose(0, 3, 1, 2, 4)
        part = part.reshape(chips, count * rows, 2 * columns)[:, :height]
        results.append(part.reshape(chips * height, 2 * columns))
    return results


def laid_out(block, rows):
    height, columns = block.shape[-2:]
    count = -(-height // rows)
    if count == 1:
        return block
    lead = block.shape[:-2]
    block = jnp.pad(block, [(0, 0)] * len(lead) + [(0, count * rows - height), (0, 0)])
    block = block.reshape(*lead, count, rows, columns)
    return jnp.moveaxis(block, -3, -2).reshape(*lead, rows, count * columns)


def joined(values, at, axis, step):
    theirs = yield swap(values, axis, step)
    first = bit_of(axis, step) == 0
    return jnp.stack([jnp.where(first, values, theirs), jnp.where(first, theirs, values)], axis=at)


def gradient_halves(values, gradient):
    flat_values = values.reshape(-1, values.shape[-1])
    flat_gradient = gradient.reshape(-1, gradient.shape[-1])
    half = flat_gradient.shape[1] // 2
    core = bit_of("rep", 1)
    other = lax.dynamic_slice_in_dim(flat_gradient, (1 - core) * half, half, 1)
    mine = lax.dynamic_slice_in_dim(flat_gradient, core * half, half, 1)
    return (
        outer_sum(flat_values, other).astype(jnp.bfloat16),
        outer_sum(flat_values, mine).astype(jnp.bfloat16),
    )


def blocks_of(shard, widths):
    half = shard.shape[1] // 2
    blocks = []
    start = 0
    for width in widths:
        size = width // 2
        pair = [shard[:, at + start : at + start + size] for at in (0, half)]
        blocks.append(jnp.concatenate(pair, axis=1))
        start += size
    return blocks


def side_by_side(*pairs):
    return tuple(jnp.concatenate(blocks, axis=1) for blocks in zip(*pairs))


def join(values, at, axis, step):
    theirs = swap(values, axis, step)
    first = bit_of(axis, step) == 0
    return jnp.stack([jnp.where(first, values, theirs), jnp.where(first, theirs, values)], axis=at)


def join_fsdp(values):
    for step in bits("fsdp"):
        values = join(values, 0, "fsdp", step)
        values = values.reshape(-1, *values.shape[2:])
    return values


def join_all(values):
    values = join_fsdp(values)
    for step in bits("rep"):
        values = join(values, 0, "rep", step)
        values = values.reshape(-1, *values.shape[2:])
    return values


def gather_rows(shard):
    part = shard.shape[0] // lax.axis_size("rep")
    mine = lax.dynamic_slice_in_dim(shard, lax.axis_index("rep") * part, part, 0)
    return lax.all_gather(mine, ("fsdp", "rep"), axis=0, tiled=True)


def part_of(shard, count, at, axis):
    size = shard.shape[axis] // count
    return lax.dynamic_slice_in_dim(shard, at * size, size, axis)


def fetch_fsdp(mine, first):
    rows, columns = mine.shape
    whole = mine[None]
    for step in reversed(bits("fsdp")[1:]):
        whole = yield from joined(whole, 1, "fsdp", step)
        whole = whole.reshape(-1, rows, columns)
    low, rep = bits("fsdp")[:1], bits("rep")[1:]
    whole = whole[:, None, None]
    for axis, step in (
        [("rep", step) for step in rep] + [("fsdp", step) for step in low]
        if first == "rep"
        else [("fsdp", step) for step in low] + [("rep", step) for step in rep]
    ):
        whole = yield from joined(whole, 1 if axis == "fsdp" else 2, axis, step)
        shape = whole.shape
        whole = (
            whole.reshape(shape[0], -1, *shape[3:])
            if axis == "fsdp"
            else whole.reshape(*shape[:2], -1, *shape[4:])
        )
    return whole.reshape(-1, whole.shape[2], rows, columns)


def exchange_rows(shard, first):
    mine = part_of(shard, lax.axis_size("rep"), lax.axis_index("rep"), 0)
    whole = yield from fetch_fsdp(mine, first)
    whole = yield from joined(whole, 2, "rep", 1)
    return whole.reshape(-1, shard.shape[1])


def exchange_columns(shard, first):
    mine = part_of(shard, 2, bit_of("rep", 1), 1)
    mine = part_of(mine, lax.axis_size("rep") // 2, lax.axis_index("rep") // 2, 0)
    whole = yield from fetch_fsdp(mine, first)
    whole = whole.reshape(-1, mine.shape[1])
    theirs = yield swap(whole, "rep", 1)
    core = bit_of("rep", 1) == 0
    return (jnp.where(core, whole, theirs), jnp.where(core, theirs, whole))


def attend(queries, key_rows, value_rows, allowed):
    scores, _ = scores_of(queries, key_rows, allowed)
    highest = jnp.max(scores, axis=-1, keepdims=True)
    exponent = jnp.exp(scores - highest)
    normalizer = jnp.sum(exponent, axis=-1, keepdims=True)
    probs = exponent / normalizer
    mixed_heads = jnp.einsum(
        "bhqk,bkhd->bqhd",
        probs.astype(jnp.bfloat16),
        split_heads(value_rows),
        preferred_element_type=jnp.float32,
    )
    mixed_heads = mixed_heads.reshape(queries.shape[0], queries.shape[1], -1).astype(jnp.bfloat16)
    return (mixed_heads, probs)


def attend_back(queries, key_rows, value_rows, attention_probs, grad_mixed):
    scaling = HEAD ** (-0.5)
    upstream = split_heads(grad_mixed)
    grad_value = jnp.einsum(
        "bhqk,bqhd->bkhd",
        attention_probs.astype(jnp.bfloat16),
        upstream,
        preferred_element_type=jnp.float32,
    )
    grad_probs = jnp.einsum(
        "bqhd,bkhd->bhqk", upstream, split_heads(value_rows), preferred_element_type=jnp.float32
    )
    grad_scores = attention_probs * (
        grad_probs - jnp.sum(attention_probs * grad_probs, axis=-1, keepdims=True)
    )
    grad_scores = grad_scores.astype(jnp.bfloat16)
    grad_query = (
        jnp.einsum(
            "bhqk,bkhd->bqhd",
            grad_scores,
            split_heads(key_rows),
            preferred_element_type=jnp.float32,
        )
        * scaling
    )
    grad_key = (
        jnp.einsum(
            "bhqk,bqhd->bkhd", grad_scores, split_heads(queries), preferred_element_type=jnp.float32
        )
        * scaling
    )
    batch = queries.shape[0]
    return (
        grad_query.reshape(batch, queries.shape[1], -1),
        grad_key.reshape(batch, key_rows.shape[1], -1),
        grad_value.reshape(batch, key_rows.shape[1], -1),
    )


def contrast(similar, reverse_sims, temper, positive, caption_total):
    image_side = jax.nn.logsumexp(similar / temper, axis=-1)
    text_side = jax.nn.logsumexp(reverse_sims / temper, axis=-1)
    matched = jnp.sum(similar * positive, axis=-1) / temper
    return jnp.sum(image_side + text_side - 2.0 * matched) / (2.0 * caption_total)


def on_device(
    sequence_entries,
    picture_descriptors,
    sentence_numbering,
    sentence_picture_owner,
    upstream_adjoint,
    attend_triple_matrix,
    inward_result_matrix,
    inward_result_offset,
    inward_center_scale,
    inward_center_shift,
    mixing_asker_matrix,
    visual_lookup_pairs,
    mixing_result_matrix,
    mixing_result_offset,
    mixing_center_scale,
    mixing_center_shift,
    widening_matrix,
    widening_offset,
    narrowing_matrix,
    narrowing_offset,
    perceptron_center_scale,
    perceptron_center_shift,
    picture_mapping_matrix,
    picture_vector_offset,
    sentence_mapping_matrix,
    sentence_vector_offset,
    logit_sharpness,
):
    f32 = jnp.float32
    bf16 = jnp.bfloat16
    everywhere = ("rep", "fsdp")
    rows, row_len, width = sequence_entries.shape
    segment_of = token_kinds(sentence_numbering)
    allowed = segment_of[:, :, None] == segment_of[:, None, :]
    picker = caption_picker(sentence_numbering)

    vectors = (
        inward_result_offset,
        inward_center_scale,
        inward_center_shift,
        mixing_result_offset,
        mixing_center_scale,
        mixing_center_shift,
        widening_offset,
        narrowing_offset,
        perceptron_center_scale,
        perceptron_center_shift,
        picture_vector_offset,
        sentence_vector_offset,
    )
    packed = join_fsdp(jnp.concatenate(vectors)[None])
    spread = []
    offset = 0
    for vector in vectors:
        size = vector.shape[0]
        spread.append(packed[:, offset : offset + size].reshape(-1).astype(f32))
        offset += size
    (
        self_offset,
        self_scale,
        self_shift,
        cross_offset,
        cross_scale,
        cross_shift,
        wide_offset,
        narrow_offset,
        feed_scale,
        feed_shift,
        image_shift,
        text_shift,
    ) = spread
    owners = join_all(sentence_picture_owner[None]).reshape(-1)

    emb = picture_mapping_matrix.shape[1]
    w_self = gather_rows(jnp.concatenate([attend_triple_matrix, inward_result_matrix], axis=1))
    w_qkv, w_self_out = w_self[:, : 3 * width], w_self[:, 3 * width :]
    w_rest = gather_rows(
        jnp.concatenate(
            [
                mixing_asker_matrix,
                mixing_result_matrix,
                widening_matrix,
                picture_mapping_matrix,
                sentence_mapping_matrix,
            ],
            axis=1,
        )
    )
    w_asker, w_cross_out = w_rest[:, :width], w_rest[:, width : 2 * width]
    w_up = w_rest[:, 2 * width : -2 * emb]
    w_image, w_text = w_rest[:, -2 * emb : -emb], w_rest[:, -emb:]
    pairs = Task(exchange_columns(visual_lookup_pairs, "rep"))
    narrow = Task(exchange_rows(narrowing_matrix, "fsdp"))
    for task in (pairs, narrow):
        while task.got is not None:
            task.advance(task.got)
    w_keys, w_values = pairs.result
    w_down = narrow.result

    qkv = project(sequence_entries, w_qkv).astype(bf16)
    q_self, k_self, v_self = (qkv[..., i * width : (i + 1) * width] for i in range(3))
    self_mix, self_probs = attend(q_self, k_self, v_self, allowed)
    first_sum = sequence_entries.astype(f32) + project(self_mix, w_self_out) + self_offset
    inner = layer_norm(first_sum, self_scale, self_shift)

    head_rows = inner[:, :QUERY]
    head_low = head_rows.astype(bf16)
    asked = project(head_low, w_asker).astype(bf16)
    k_cross = project(picture_descriptors, w_keys).astype(bf16)
    v_cross = project(picture_descriptors, w_values).astype(bf16)
    cross_mix, cross_probs = attend(asked, k_cross, v_cross, None)
    second_sum = head_rows + project(cross_mix, w_cross_out) + cross_offset
    normed = layer_norm(second_sum, cross_scale, cross_shift)
    merged = jnp.concatenate([normed, inner[:, QUERY:]], axis=1)

    merged_low = merged.astype(bf16)
    pre_act = project(merged_low, w_up) + wide_offset
    activated = exact_gelu(pre_act).astype(bf16)
    third_sum = merged + project(activated, w_down) + narrow_offset
    final = layer_norm(third_sum, feed_scale, feed_shift)
    out = final.astype(bf16)

    pooled_low = jnp.mean(final[:, :QUERY], axis=1).astype(bf16)
    image_raw = project(pooled_low, w_image) + image_shift
    image_unit = unit_rows(image_raw).astype(bf16)
    caption_low = jnp.einsum(
        "rcp,rpd->rcd", picker.astype(bf16), out[:, QUERY:], preferred_element_type=f32
    )
    caption_low = caption_low.astype(bf16).reshape(-1, width)
    text_raw = project(caption_low, w_text) + text_shift
    text_unit = unit_rows(text_raw).astype(bf16)
    units = join_all(jnp.concatenate([image_unit, text_unit], axis=0)[None])
    all_images = units[:, :rows].reshape(-1, emb)
    all_texts = units[:, rows:].reshape(-1, emb)
    image_total = all_images.shape[0]
    text_total = all_texts.shape[0]
    positive = owners[:, None] == jnp.arange(image_total, dtype=jnp.int32)[None, :]
    similar = lax.dot_general(
        all_texts, all_images, (((1,), (1,)), ((), ())), preferred_element_type=f32
    )
    chosen = jnp.dot(positive.astype(bf16), all_images, preferred_element_type=f32).astype(bf16)
    reverse_sims = lax.dot_general(
        chosen, all_texts, (((1,), (1,)), ((), ())), preferred_element_type=f32
    )
    _, contrast_pull = jax.vjp(
        partial(contrast, positive=positive.astype(f32), caption_total=text_total),
        similar,
        reverse_sims,
        logit_sharpness,
    )
    grad_sims, grad_back, sharpness_adjoint = contrast_pull(jnp.ones((), f32))
    grad_sims = grad_sims.astype(bf16)
    grad_back = grad_back.astype(bf16)
    device = lax.axis_index("rep") * lax.axis_size("fsdp") + lax.axis_index("fsdp")
    texts_here = text_unit.shape[0]
    grad_chosen = jnp.dot(grad_back, all_texts, preferred_element_type=f32)
    own_images = device * rows + jnp.arange(rows, dtype=jnp.int32)
    own_positive = (owners[:, None] == own_images[None, :]).astype(f32)
    own_columns = lax.dynamic_slice_in_dim(grad_sims, device * rows, rows, 1)
    grad_image_unit = outer_sum(own_columns, all_texts) + lax.dot_general(
        own_positive,
        grad_chosen,
        (((0,), (0,)), ((), ())),
        precision=lax.Precision.HIGHEST,
        preferred_element_type=f32,
    )
    own_rows = lax.dynamic_slice_in_dim(grad_sims, device * texts_here, texts_here, 0)
    own_back = lax.dynamic_slice_in_dim(grad_back, device * texts_here, texts_here, 1)
    grad_text_unit = jnp.dot(own_rows, all_images, preferred_element_type=f32) + outer_sum(
        own_back, chosen
    )
    _, image_pull = jax.vjp(unit_rows, image_raw)
    grad_image_raw = image_pull(grad_image_unit)[0].astype(bf16)
    _, text_pull = jax.vjp(unit_rows, text_raw)
    grad_text_raw = text_pull(grad_text_unit)[0].astype(bf16)
    grad_pooled = project_back(grad_image_raw, w_image) / QUERY
    grad_captions = project_back(grad_text_raw, w_text).reshape(rows, CAPS_ROW, width)
    grad_caption_rows = jnp.sum(picker[:, :, :, None] * grad_captions[:, :, None, :], axis=1)
    grad_query_rows = jnp.broadcast_to(grad_pooled[:, None, :], (rows, QUERY, width))
    grad_final = upstream_adjoint.astype(f32) + jnp.concatenate(
        [grad_query_rows, grad_caption_rows], axis=1
    )

    grad_third_sum, feed_gain, feed_shift_grad = norm_back(
        third_sum, feed_scale, feed_shift, grad_final
    )
    grad_third = grad_third_sum.astype(bf16)
    down = Task(flow(*gradient_halves(activated, grad_third), "fsdp"))
    grad_active = project_back(grad_third, w_down)
    _, gelu_pull = jax.vjp(exact_gelu, pre_act)
    grad_pre = gelu_pull(grad_active)[0].astype(bf16)
    grad_pre = tie(grad_pre, down)
    ends = jnp.concatenate(
        [outer_sum(pooled_low, grad_image_raw), outer_sum(caption_low, grad_text_raw)], axis=1
    ).astype(bf16)
    ends_halves = (part_of(ends, 2, 1 - bit_of("rep", 1), 1), part_of(ends, 2, bit_of("rep", 1), 1))
    up = Task(flow(*side_by_side(gradient_halves(merged_low, grad_pre), ends_halves), "rep"))
    grad_merged = grad_third_sum + project_back(grad_pre, w_up)
    grad_merged = tie(grad_merged, up)

    grad_second_sum, cross_gain, cross_shift_grad = norm_back(
        second_sum, cross_scale, cross_shift, grad_merged[:, :QUERY]
    )
    grad_second = grad_second_sum.astype(bf16)
    grad_cross_mix = project_back(grad_second, w_cross_out).astype(bf16)
    cross_out_halves = gradient_halves(cross_mix, grad_second)
    grad_asked, grad_key, grad_value = attend_back(
        asked, k_cross, v_cross, cross_probs, grad_cross_mix
    )
    grad_asked = grad_asked.astype(bf16)
    grad_asked = tie(grad_asked, down, up)
    core_zero = bit_of("rep", 1) == 0
    grad_key = grad_key.astype(bf16)
    grad_value = grad_value.astype(bf16)
    keyval = Task(flow(
        outer_sum(picture_descriptors, jnp.where(core_zero, grad_value, grad_key)).astype(bf16),
        outer_sum(picture_descriptors, jnp.where(core_zero, grad_key, grad_value)).astype(bf16),
        "fsdp",
    ))
    asker_halves = gradient_halves(head_low, grad_asked)
    grad_head = grad_second_sum + project_back(grad_asked, w_asker)
    grad_inner = jnp.concatenate([grad_head, grad_merged[:, QUERY:]], axis=1)
    grad_inner = tie(grad_inner, keyval)

    grad_first_sum, self_gain, self_shift_grad = norm_back(
        first_sum, self_scale, self_shift, grad_inner
    )
    grad_first = grad_first_sum.astype(bf16)
    middle = Task(flow(
        *side_by_side(cross_out_halves, asker_halves, gradient_halves(self_mix, grad_first)), "rep"
    ))
    grad_self_mix = project_back(grad_first, w_self_out).astype(bf16)
    grad_self_mix = tie(grad_self_mix, down, up, middle)
    grad_q, grad_k, grad_v = attend_back(q_self, k_self, v_self, self_probs, grad_self_mix)
    grad_q = tie(grad_q, keyval)
    grad_v = tie(grad_v, middle)
    grad_qkv = jnp.concatenate([grad_q, grad_k, grad_v], axis=-1).astype(bf16)
    vector_grads = (
        column_sum(grad_pre),
        column_sum(grad_third),
        feed_gain,
        feed_shift_grad,
        column_sum(grad_second),
        cross_gain,
        cross_shift_grad,
        column_sum(grad_image_raw),
        column_sum(grad_text_raw),
        column_sum(grad_first),
        self_gain,
        self_shift_grad,
    )
    fsdp = lax.axis_size("fsdp")
    chips = lax.axis_size("rep") // 2
    share = width // fsdp
    packed = jnp.concatenate([vector.reshape(fsdp, -1) for vector in vector_grads], axis=1)
    lanes = 128
    slots = -(-packed.shape[1] // (2 * chips * lanes))
    assert slots <= share // chips
    packed = jnp.pad(packed, [(0, 0), (0, 2 * chips * slots * lanes - packed.shape[1])])
    packed = packed.astype(bf16).reshape(fsdp, 2, chips, slots, lanes)
    packed = jnp.pad(packed, [(0, 0)] * 3 + [(0, share // chips - slots), (0, 0)])
    packed = jnp.moveaxis(packed, 1, 0).reshape(2, width, lanes)
    core = bit_of("rep", 1)
    packed_halves = tuple(
        lax.dynamic_index_in_dim(packed, at, 0, False) for at in (1 - core, core)
    )
    last = Task(
        flow(*side_by_side(gradient_halves(sequence_entries, grad_qkv), packed_halves), "fsdp")
    )
    incoming = grad_first_sum + project_back(grad_qkv, w_qkv)
    rows_here = share // chips
    lockstep(last, keyval, middle)
    early = Task(shards((up.result, down.result, keyval.result), rows_here))
    while last.got is not None:
        lockstep(last, early)
    late = Task(shards((middle.result, last.result), rows_here))
    while late.got is not None or early.got is not None:
        lockstep(late, early)
    up_shard, down_shard, keyval_shard = early.result
    middle_shard, last_shard = late.result
    up_grad, ends_grad = blocks_of(up_shard, (widening_matrix.shape[1], 2 * emb))
    cross_out_grad, asker_grad, self_out_grad = blocks_of(middle_shard, (width,) * 3)
    qkv_grad, packed = blocks_of(last_shard, (3 * width, 2 * lanes))
    packed = packed.reshape(chips, rows_here, 2, lanes)[:, :slots]
    packed = jnp.moveaxis(packed, 2, 0).reshape(-1)
    vector_shards = []
    offset = 0
    for vector in vector_grads:
        size = vector.shape[0] // fsdp
        vector_shards.append(packed[offset : offset + size])
        offset += size
    (
        up_bias,
        down_bias,
        feed_gain,
        feed_shift_grad,
        cross_bias,
        cross_gain,
        cross_shift_grad,
        image_bias,
        text_bias,
        self_bias,
        self_gain,
        self_shift_grad,
    ) = vector_shards
    return (
        out,
        incoming,
        qkv_grad,
        self_out_grad,
        self_bias,
        self_gain,
        self_shift_grad,
        asker_grad,
        keyval_shard,
        cross_out_grad,
        cross_bias,
        cross_gain,
        cross_shift_grad,
        up_grad,
        up_bias,
        down_shard,
        down_bias,
        feed_gain,
        feed_shift_grad,
        ends_grad[:, :emb],
        image_bias,
        ends_grad[:, emb:],
        text_bias,
        sharpness_adjoint,
    )


def solution(mesh):
    placed = (
        P(("rep", "fsdp"), None, None),
        P(("rep", "fsdp"), None, None),
        P(("rep", "fsdp"), None),
        P(("rep", "fsdp")),
        P(("rep", "fsdp"), None, None),
        P("fsdp", None),
        P("fsdp", None),
        P("fsdp"),
        P("fsdp"),
        P("fsdp"),
        P("fsdp", None),
        P("fsdp", None),
        P("fsdp", None),
        P("fsdp"),
        P("fsdp"),
        P("fsdp"),
        P("fsdp", None),
        P("fsdp"),
        P("fsdp", None),
        P("fsdp"),
        P("fsdp"),
        P("fsdp"),
        P("fsdp", None),
        P("fsdp"),
        P("fsdp", None),
        P("fsdp"),
        P(),
    )
    return jax.shard_map(
        on_device,
        mesh=mesh,
        in_specs=placed,
        out_specs=(
            P(("rep", "fsdp"), None, None),
            P(("rep", "fsdp"), None, None),
            P("fsdp", None),
            P("fsdp", None),
            P("fsdp"),
            P("fsdp"),
            P("fsdp"),
            P("fsdp", None),
            P("fsdp", None),
            P("fsdp", None),
            P("fsdp"),
            P("fsdp"),
            P("fsdp"),
            P("fsdp", None),
            P("fsdp"),
            P("fsdp", None),
            P("fsdp"),
            P("fsdp"),
            P("fsdp"),
            P("fsdp", None),
            P("fsdp"),
            P("fsdp", None),
            P("fsdp"),
            P(),
        ),
        check_vma=False,
    )
```
